32 devices in a mesh: groups: 2 (over x), hid: 8 (over z, y), wid: 2 (over core).
Axes of the slice: x: 2, y: 2, z: 4, core: 2. Of those that a mesh axis runs over, the one named last changes fastest.
Arguments:
- tokens: bfloat16 [256, 18432], P(('groups', 'hid'), 'wid'), parts along dimension 0, may hold values from -180 to 180
- norm_gain: float32 [18432], P('wid'), may hold values from 0.1 to 1.9
- query_weight: bfloat16 [18432, 8192], P('wid', 'hid'), may hold values from -0.046875 to 0.046875
- query_scale: float32 [8192], P('hid'), may hold values from 0.5 to 2
- kv_weight: bfloat16 [18432, 512], P('wid'), may hold values from -0.046875 to 0.046875
- kv_scale: float32 [512], replicated, may hold values from 0.5 to 2
- keys_cache: bfloat16 [256, 512, 256], P(('groups', 'hid', 'wid')), parts along dimension 0, may hold values from -384 to 384
- values_cache: bfloat16 [256, 512, 256], P(('groups', 'hid', 'wid')), parts along dimension 0, may hold values from -6 to 6
- lengths: int32 [256], P(('groups', 'hid', 'wid')), parts along dimension 0, may hold values from 1 to 512, as said below
Outputs:
- attended: bfloat16 [256, 8192], P(('groups', 'hid', 'wid')), parts along dimension 0
- new_entries: bfloat16 [256, 512], P(('groups', 'hid', 'wid')), parts along dimension 0
The draws below stay inside these ranges and needn't reach their ends.
There are 2 independent parts, one for each index of `groups`. The reference program is written for one: setup_inputs(seed, part) draws one part's arguments, and reference() takes and returns one part's arrays. A program takes and returns all parts, laid end to end along the dimension named above; an argument that names none is the same for every part. Nothing has to cross between parts.
Inputs may be any that keep to these rules, and one draw needn't show every extreme that they name: `lengths`: in one aligned block of 8 requests every length is 512.
All inputs are finite; a program needn't handle non-finite values.
Results may differ from the reference program's by a relative error of at most 0.009.
The reference program's roundings to bfloat16 on the way count: a program that leaves them out, or rounds other values in their place, can miss the bound.
Values may be sent and summed in bfloat16 or wider, within the bound.
A program may use at most 128 MiB of HBM per device.

```python
import math
import jax
import jax.numpy as jnp
from jax import lax

D = 18432
HEADS = 32
HD = 256
REQ_DEV = 8
CACHE = 512
BATCH = 128


def draw_tokens(key, part):
    key_rows, key_cols, key_base = jax.random.split(key, 3)
    row_scale = jnp.exp(jax.random.uniform(key_rows, (BATCH, 1), minval=0.0, maxval=math.log(10.0)))
    col_scale = jnp.exp(jax.random.uniform(key_cols, (1, D), minval=math.log(0.3), maxval=math.log(3.0)))
    base_values = jnp.clip(jax.random.normal(key_base, (BATCH, D)), -6.0, 6.0)
    return (base_values * col_scale * row_scale).astype(jnp.bfloat16)


def draw_keys_cache(key, part):
    key_base = jax.random.fold_in(key, 0)
    base_values = jnp.clip(jax.random.normal(key_base, (BATCH, CACHE, HD)), -6.0, 6.0)
    return base_values.astype(jnp.bfloat16)


def draw_lengths(key, part):
    key_len, key_block = jax.random.split(key)
    drawn_lengths = jax.random.randint(key_len, (BATCH,), 1, CACHE + 1)
    full_block = jax.random.randint(key_block, (), 0, BATCH // REQ_DEV)
    row_block = jnp.arange(BATCH) // REQ_DEV
    return jnp.where(row_block == full_block, CACHE, drawn_lengths).astype(jnp.int32)


def levels(stream_key, shape, cuts, least, high):
    def one(axis_at, parts):
        heights = jax.random.uniform(jax.random.fold_in(jax.random.fold_in(stream_key, 6), axis_at), (parts,), jnp.float32, least / len(cuts), high / len(cuts))
        return jnp.repeat(jnp.exp(heights), shape[axis_at] // parts).reshape((-1,) + (1,) * (len(shape) - axis_at - 1))

    level = one(*cuts[0])
    for cut in cuts[1:]:
        level = level * one(*cut)
    return level


def normal_values(key, extent, spread, reach, shards=(), kind=jnp.bfloat16):
    values = spread * jax.random.normal(key, extent, jnp.float32)
    if shards:
        values = values * levels(key, extent, shards, -0.22, 0.18)
    return jnp.clip(values, -reach, reach).astype(kind)


def setup_inputs(seed: int = 0, part: int = 0) -> dict:
    seeds = jax.random.split(jax.random.key(seed), 10)
    own_keys = jax.random.split(jax.random.fold_in(seeds[9], part), 10)
    return {
        "tokens": draw_tokens(jax.random.fold_in(jax.random.fold_in(seeds[9], part), 71), part),
        "norm_gain": jnp.clip(1.0 + 0.18 * jax.random.normal(seeds[1], (D,), jnp.float32), 0.1, 1.9),
        "query_weight": normal_values(seeds[2], (D, HEADS * HD), D ** -0.5, 0.046875, ((0, 2), (1, 8))),
        "query_scale": jnp.clip(jnp.exp(math.log(2.0) - 1.3862944 * jax.random.uniform(seeds[3], (HEADS * HD,), jnp.float32) ** levels(seeds[3], (HEADS * HD,), ((0, 8),), -0.2, 0.2)), 0.5, 2.0),
        "kv_weight": normal_values(seeds[4], (D, 2 * HD), D ** -0.5, 0.046875, ((0, 2),)),
        "kv_scale": jnp.clip(jnp.exp(jax.random.uniform(seeds[5], (2 * HD,), jnp.float32, math.log(0.5), math.log(2.0))), 0.5, 2.0),
        "keys_cache": draw_keys_cache(jax.random.fold_in(jax.random.fold_in(seeds[9], part), 71), part),
        "values_cache": normal_values(own_keys[7], (BATCH, CACHE, HD), 1.0, 6.0, ((0, 16),)),
        "lengths": draw_lengths(jax.random.fold_in(jax.random.fold_in(seeds[9], part), 71), part),
    }


EPSILON = 1e-05

def attend_all(queries, new_entries, keys_cache, values_cache, lengths):
    row_count, cache_len, head_dim = keys_cache.shape
    head_count = queries.shape[1] // head_dim
    query_heads = queries.reshape(row_count, head_count, head_dim).astype(jnp.float32)
    new_keys = new_entries[:, :head_dim].astype(jnp.float32)
    new_values = new_entries[:, head_dim:].astype(jnp.float32)
    inv_root = head_dim ** (-0.5)
    cache_scores = jnp.einsum('rhd,rtd->rht', query_heads, keys_cache.astype(jnp.float32)) * inv_root
    positions = lax.broadcasted_iota(jnp.int32, (row_count, 1, cache_len), 2)
    is_live = positions < lengths.astype(jnp.int32)[:, None, None]
    cache_scores = jnp.where(is_live, cache_scores, -jnp.inf)
    own_scores = jnp.einsum('rhd,rd->rh', query_heads, new_keys) * inv_root
    peak_score = jnp.maximum(lax.optimization_barrier(jnp.max(cache_scores, axis=2)), own_scores)
    cache_exp = jnp.exp(cache_scores - peak_score[:, :, None])
    own_exp = jnp.exp(own_scores - peak_score)
    denom_sum = lax.optimization_barrier(jnp.sum(cache_exp, axis=2)) + own_exp
    cache_weights = (cache_exp / denom_sum[:, :, None]).astype(jnp.bfloat16)
    own_weights = (own_exp / denom_sum).astype(jnp.bfloat16)
    blended = jnp.einsum('rht,rtd->rhd', cache_weights.astype(jnp.float32), values_cache.astype(jnp.float32))
    blended = blended + own_weights.astype(jnp.float32)[:, :, None] * new_values[:, None, :]
    return blended.reshape(row_count, head_count * head_dim).astype(jnp.bfloat16)

def reference(tokens, norm_gain, query_weight, query_scale, kv_weight, kv_scale, keys_cache, values_cache, lengths):
    row_values = tokens.astype(jnp.float32)
    row_mean = lax.optimization_barrier(jnp.mean(row_values, axis=1))
    variance = lax.optimization_barrier(jnp.mean(row_values * row_values, axis=1)) - row_mean * row_mean
    normed = ((row_values - row_mean[:, None]) * lax.rsqrt(variance + EPSILON)[:, None] * norm_gain.astype(jnp.float32)).astype(jnp.bfloat16)
    queries = (jnp.dot(normed, query_weight, preferred_element_type=jnp.float32) * query_scale.astype(jnp.float32)).astype(jnp.bfloat16)
    new_entries = (jnp.dot(normed, kv_weight, preferred_element_type=jnp.float32) * kv_scale.astype(jnp.float32)).astype(jnp.bfloat16)
    attended = attend_all(queries, new_entries, keys_cache, values_cache, lengths)
    return (attended, new_entries)
```

```python
import functools

import jax
import jax.numpy as jnp
from jax import lax
from jax.experimental import pallas as pl
from jax.experimental.pallas import tpu as pltpu
from jax.sharding import PartitionSpec as P

EPSILON = 1e-05
CHUNKS = 6
ROWS_Y = 2
UP, DOWN, SIDE = 0, 1, 2
MESH = pl.DeviceIdType.MESH


def kernel(
    hid_count, wid_count,
    tok_hbm, gain_hbm, qw_hbm, qs_hbm, kw_hbm, ks_hbm, keys_hbm, vals_hbm, len_ref,
    att_ref, new_ref,
    gat, gain, qw, qs, kw, ks, keys, vals,
    stat_mine, stat_other, stats, normed, acc, acc_rx, kv_acc, kv_rx, kv_new,
    q_tx, q_rx, q_f32, o_f32, att,
    tok_sem, qw_sem, kw_sem, misc_sem,
    send_sem, recv_sem, pair_sem, stat_send, stat_recv, acc_send, acc_recv, q_send, q_recv, out_sem,
):
    own_rows, half_width = tok_hbm.shape
    full_width = half_width * wid_count
    width = half_width // CHUNKS
    tiles, _, _, req, head_dim = acc.shape
    z_count = hid_count // ROWS_Y
    me = lax.axis_index("hid")
    core = lax.axis_index("wid")
    other = 1 - core
    z = me // ROWS_Y
    y = lax.rem(me, ROWS_Y)
    side = z * ROWS_Y + (1 - y)

    def hid_at(zz, yy):
        return zz * ROWS_Y + yy

    def cols(c):
        return pl.ds(pl.multiple_of(c * width, 128), width)

    def tok_copy(c):
        return pltpu.make_async_copy(tok_hbm.at[:, cols(c)], gat.at[me, c], tok_sem.at[c])

    def kw_copy(c):
        return pltpu.make_async_copy(kw_hbm.at[cols(c)], kw.at[c], kw_sem.at[c])

    def qw_copy(c):
        return pltpu.make_async_copy(qw_hbm.at[cols(c)], qw.at[c], qw_sem.at[c])

    small = [
        pltpu.make_async_copy(gain_hbm, gain, misc_sem.at[0]),
        pltpu.make_async_copy(qs_hbm, qs, misc_sem.at[1]),
        pltpu.make_async_copy(ks_hbm, ks, misc_sem.at[2]),
        pltpu.make_async_copy(keys_hbm, keys, misc_sem.at[3]),
        pltpu.make_async_copy(vals_hbm, vals, misc_sem.at[4]),
    ]
    for c in range(CHUNKS):
        tok_copy(c).start()
    for copy in small[:3]:
        copy.start()

    barrier = pltpu.get_barrier_semaphore()
    for d in range(1, hid_count):
        pl.semaphore_signal(
            barrier, inc=1, device_id={"hid": lax.rem(me + d, hid_count)}, device_id_type=MESH
        )
    pl.semaphore_signal(barrier, inc=1, device_id={"wid": other}, device_id_type=MESH)
    for c in range(CHUNKS):
        kw_copy(c).start()
    for c in range(CHUNKS):
        qw_copy(c).start()
    for copy in small[3:]:
        copy.start()

    row_sum = jnp.zeros((own_rows, 1), jnp.float32)
    row_squares = jnp.zeros((own_rows, 1), jnp.float32)
    for c in range(CHUNKS):
        tok_copy(c).wait()
        block = gat[me, c].astype(jnp.float32)
        row_sum += jnp.sum(block, axis=1, keepdims=True)
        row_squares += jnp.sum(block * block, axis=1, keepdims=True)
    lane = lax.broadcasted_iota(jnp.int32, (own_rows, 128), 1)
    stat_mine[...] = jnp.where(lane < 64, row_sum, row_squares)

    pl.semaphore_wait(barrier, hid_count)

    def send(h, c, link):
        if link == UP:
            target = hid_at(z + 1, y)
        elif link == DOWN:
            target = hid_at(z - 1, y)
        else:
            target = side
        return pltpu.make_async_remote_copy(
            src_ref=gat.at[h, c], dst_ref=gat.at[h, c],
            send_sem=send_sem.at[link, h, c], recv_sem=recv_sem.at[h, c],
            device_id={"hid": target}, device_id_type=MESH,
        )

    def arrived(h, c):
        pltpu.make_async_remote_copy(
            src_ref=gat.at[h, c], dst_ref=gat.at[h, c],
            send_sem=send_sem.at[SIDE, h, c], recv_sem=recv_sem.at[h, c],
            device_id={"hid": side}, device_id_type=MESH,
        ).wait_recv()

    def pair(src, dst, k):
        return pltpu.make_async_remote_copy(
            src_ref=src, dst_ref=dst, send_sem=pair_sem.at[0, k], recv_sem=pair_sem.at[1, k],
            device_id={"wid": other}, device_id_type=MESH,
        )

    def own_sends(c, act):
        @pl.when(z + 1 < z_count)
        def _():
            act(send(me, c, UP))

        @pl.when(z > 0)
        def _():
            act(send(me, c, DOWN))

        act(send(me, c, SIDE))

    start = lambda copy: copy.start()
    stat_pair = pair(stat_mine, stat_other, 0)
    stat_pair.start()
    own_sends(0, start)
    own_sends(1, start)
    stat_pair.wait()
    both = stat_mine[...] + stat_other[...]
    row_mean = both[:, 0:1] / full_width
    variance = both[:, 64:65] / full_width - row_mean * row_mean
    stats[me] = jnp.where(lane < 64, row_mean, lax.rsqrt(variance + EPSILON))

    def stat_copy(d):
        target = lax.rem(me + d, hid_count)
        return pltpu.make_async_remote_copy(
            src_ref=stats.at[me], dst_ref=stats.at[me],
            send_sem=stat_send.at[d], recv_sem=stat_recv.at[me],
            device_id={"hid": target}, device_id_type=MESH,
        )

    def stat_arrived(h):
        pltpu.make_async_remote_copy(
            src_ref=stats.at[h], dst_ref=stats.at[h],
            send_sem=stat_send.at[0], recv_sem=stat_recv.at[h],
            device_id={"hid": side}, device_id_type=MESH,
        ).wait_recv()

    for d in range(1, hid_count):
        stat_copy(d).start()
    for c in range(2, CHUNKS):
        own_sends(c, start)

    for copy in small[:3]:
        copy.wait()

    def normalised(h, c):
        stat = stats[h]
        block = gat[h, c].astype(jnp.float32)
        return ((block - stat[:, 0:1]) * stat[:, 64:65] * gain[:, cols(c)]).astype(jnp.bfloat16)

    kv_acc[...] = jnp.zeros_like(kv_acc)

    def kv_step(c, carry):
        kw_copy(c).wait()
        part = jnp.dot(normalised(me, c), kw[c], preferred_element_type=jnp.float32)
        kv_acc[...] += part.reshape(kv_acc.shape)
        return carry

    lax.fori_loop(0, CHUNKS, kv_step, 0)
    kv_pair = pair(kv_acc.at[other], kv_rx, 1)
    kv_pair.start()

    acc[...] = jnp.zeros_like(acc)

    def for_sources(visit):
        for k in range(1, z_count):
            @pl.when(z - k >= 0)
            def _():
                visit(z - k, UP)

            @pl.when(z + k < z_count)
            def _():
                visit(z + k, DOWN)

    def onward(h, c, link, act):
        if link == UP:
            @pl.when(z + 1 < z_count)
            def _():
                act(send(h, c, UP))
        else:
            @pl.when(z > 0)
            def _():
                act(send(h, c, DOWN))

    def relay(c, act, wait):
        def visit(zz, link):
            h = hid_at(zz, y)
            if wait:
                arrived(h, c)
            onward(h, c, link, act)
            act(send(h, c, SIDE))

        for_sources(visit)

    def relay_last(c, act, wait):
        if wait:
            arrived(side, c)
        onward(side, c, UP, act)
        onward(side, c, DOWN, act)

        def visit(zz, link):
            for yy in (y, 1 - y):
                h = hid_at(zz, yy)
                if wait:
                    arrived(h, c)
                onward(h, c, link, act)

        for_sources(visit)

    def arrived_side(c):
        arrived(side, c)

        def visit(zz, link):
            arrived(hid_at(zz, 1 - y), c)

        for_sources(visit)

    def normalise_all(c):
        def one(h, carry):
            normed[pl.ds(pl.multiple_of(h * own_rows, own_rows), own_rows), :] = normalised(h, c)
            return carry

        lax.fori_loop(0, hid_count, one, 0)

    def product(c, n):
        columns = pl.ds(n * head_dim, head_dim)
        part = jnp.dot(normed[...], qw[c, :, columns], preferred_element_type=jnp.float32)
        return part.reshape(acc.shape[1:])

    def compute(c):
        normalise_all(c)
        qw_copy(c).wait()
        for n in range(tiles):
            acc[n] += product(c, n)

    last = CHUNKS - 1
    relay(0, start, True)
    for d in range(1, hid_count):
        stat_arrived(lax.rem(me + d, hid_count))

    def step(c, carry):
        relay(c, start, True)
        arrived_side(c - 1)
        compute(c - 1)
        return carry

    lax.fori_loop(1, last, step, 0)
    kv_pair.wait()
    kv_new[...] = ((kv_acc[core] + kv_rx[...]) * ks[...]).astype(jnp.bfloat16)
    new_out = pltpu.make_async_copy(kv_new, new_ref, out_sem.at[0])
    new_out.start()
    relay_last(last, start, True)
    arrived_side(last - 1)
    compute(last - 1)

    def acc_copy(n):
        return pltpu.make_async_remote_copy(
            src_ref=acc.at[n, :, other], dst_ref=acc_rx.at[n],
            send_sem=acc_send.at[n], recv_sem=acc_recv.at[n],
            device_id={"wid": other}, device_id_type=MESH,
        )

    def q_copy(n, d):
        target = lax.rem(me + d, hid_count)
        return pltpu.make_async_remote_copy(
            src_ref=q_tx.at[n, target], dst_ref=q_rx.at[me * tiles + n],
            send_sem=q_send.at[n, d], recv_sem=q_recv.at[me * tiles + n],
            device_id={"hid": target}, device_id_type=MESH,
        )

    def q_arrived(h, n):
        pltpu.make_async_remote_copy(
            src_ref=q_tx.at[n, h], dst_ref=q_rx.at[h * tiles + n],
            send_sem=q_send.at[n, 0], recv_sem=q_recv.at[h * tiles + n],
            device_id={"hid": side}, device_id_type=MESH,
        ).wait_recv()

    normalise_all(last)
    qw_copy(last).wait()
    for n in range(tiles):
        acc[n] += product(last, n)
        acc_copy(n).start()
    for n in range(tiles):
        acc_copy(n).wait_recv()
        total = acc[n, :, core] + acc_rx[n]
        scale = qs[:, pl.ds(n * head_dim, head_dim)]
        q_tx[n] = (total * scale[None]).astype(jnp.bfloat16)
        for d in range(1, hid_count):
            q_copy(n, d).start()
        q_rx[me * tiles + n] = q_tx[n, me]

    finish = lambda copy: copy.wait_send()

    def drain(c, carry):
        own_sends(c, finish)
        return carry

    lax.fori_loop(0, CHUNKS, drain, 0)

    def drain_relay(c, carry):
        relay(c, finish, False)
        return carry

    lax.fori_loop(0, last, drain_relay, 0)
    relay_last(last, finish, False)
    for d in range(1, hid_count):
        stat_copy(d).wait_send()
    for copy in small[3:]:
        copy.wait()

    for n in range(tiles):
        for d in range(1, hid_count):
            q_arrived(lax.rem(me + d, hid_count), n)

    heads = hid_count * tiles
    cache_len = keys.shape[1]
    inv_root = head_dim ** (-0.5)
    q_f32[...] = q_rx[...].astype(jnp.float32)
    position = lax.broadcasted_iota(jnp.int32, (heads, cache_len), 1)
    entries = kv_new[...].astype(jnp.float32)
    for r in range(req):
        query = q_f32[:, r, :]
        score = lax.dot_general(
            query.astype(jnp.bfloat16), keys[r], (((1,), (1,)), ((), ())),
            preferred_element_type=jnp.float32,
        ) * inv_root
        score = jnp.where(position < len_ref[r], score, -jnp.inf)
        own = jnp.sum(query * entries[r : r + 1, :head_dim], axis=1, keepdims=True) * inv_root
        peak = jnp.maximum(jnp.max(score, axis=1, keepdims=True), own)
        weight = jnp.exp(score - peak)
        own_weight = jnp.exp(own - peak)
        denom = jnp.sum(weight, axis=1, keepdims=True) + own_weight
        weight = (weight / denom).astype(jnp.bfloat16)
        own_weight = (own_weight / denom).astype(jnp.bfloat16).astype(jnp.float32)
        mixed = jnp.dot(weight, vals[r], preferred_element_type=jnp.float32)
        o_f32[:, r, :] = mixed + own_weight * entries[r : r + 1, head_dim:]
    for h in range(heads):
        att[:, h * head_dim : (h + 1) * head_dim] = o_f32[h].astype(jnp.bfloat16)
    att_out = pltpu.make_async_copy(att, att_ref, out_sem.at[1])
    att_out.start()
    for n in range(tiles):
        acc_copy(n).wait_send()
        for d in range(1, hid_count):
            q_copy(n, d).wait_send()
    new_out.wait()
    att_out.wait()


def body(
    tokens, norm_gain, query_weight, query_scale, kv_weight, kv_scale,
    keys_cache, values_cache, lengths,
):
    hid_count = lax.axis_size("hid")
    wid_count = lax.axis_size("wid")
    own_rows, half_width = tokens.shape
    local_cols = query_weight.shape[1]
    req, cache_len, head_dim = keys_cache.shape
    tiles = local_cols // head_dim
    heads = hid_count * tiles
    width = half_width // CHUNKS
    kv_cols = kv_weight.shape[1]
    bf16, f32 = jnp.bfloat16, jnp.float32
    dma = pltpu.SemaphoreType.DMA
    vm = pltpu.VMEM
    scratch = [
        vm((hid_count, CHUNKS, own_rows, width), bf16),
        vm((1, half_width), f32),
        vm((CHUNKS, width, local_cols), bf16),
        vm((1, local_cols), f32),
        vm((CHUNKS, width, kv_cols), bf16),
        vm((1, kv_cols), f32),
        vm(keys_cache.shape, bf16),
        vm(values_cache.shape, bf16),
        vm((own_rows, 128), f32),
        vm((own_rows, 128), f32),
        vm((hid_count, own_rows, 128), f32),
        vm((hid_count * own_rows, width), bf16),
        vm((tiles, hid_count, wid_count, req, head_dim), f32),
        vm((tiles, hid_count, req, head_dim), f32),
        vm((wid_count, req, kv_cols), f32),
        vm((req, kv_cols), f32),
        vm((req, kv_cols), bf16),
        vm((tiles, hid_count, req, head_dim), bf16),
        vm((heads, req, head_dim), bf16),
        vm((heads, req, head_dim), f32),
        vm((heads, req, head_dim), f32),
        vm((req, heads * head_dim), bf16),
        dma((CHUNKS,)),
        dma((CHUNKS,)),
        dma((CHUNKS,)),
        dma((5,)),
        dma((3, hid_count, CHUNKS)),
        dma((hid_count, CHUNKS)),
        dma((2, 2)),
        dma((hid_count,)),
        dma((hid_count,)),
        dma((tiles,)),
        dma((tiles,)),
        dma((tiles, hid_count)),
        dma((heads,)),
        dma((2,)),
    ]
    hbm = pl.BlockSpec(memory_space=pl.ANY)
    return pl.pallas_call(
        functools.partial(kernel, hid_count, wid_count),
        out_shape=(
            jax.ShapeDtypeStruct((req, heads * head_dim), bf16),
            jax.ShapeDtypeStruct((req, kv_cols), bf16),
        ),
        in_specs=[hbm] * 8 + [pl.BlockSpec(memory_space=pltpu.SMEM)],
        out_specs=(hbm, hbm),
        scratch_shapes=scratch,
        compiler_params=pltpu.CompilerParams(
            collective_id=0, has_side_effects=True, vmem_limit_bytes=60 * 1024 * 1024
        ),
    )(
        tokens, norm_gain.reshape(1, -1), query_weight, query_scale.reshape(1, -1),
        kv_weight, kv_scale.reshape(1, -1), keys_cache, values_cache, lengths,
    )


def solution(mesh):
    placed = (
        P(("groups", "hid"), "wid"),
        P("wid"),
        P("wid", "hid"),
        P("hid"),
        P("wid", None),
        P(),
        P(("groups", "hid", "wid"), None, None),
        P(("groups", "hid", "wid"), None, None),
        P(("groups", "hid", "wid")),
    )
    return jax.shard_map(
        body,
        mesh=mesh,
        in_specs=placed,
        out_specs=(P(("groups", "hid", "wid"), None), P(("groups", "hid", "wid"), None)),
        check_vma=False,
    )
```

```python
import functools

import jax
import jax.numpy as jnp
from jax import lax
from jax.experimental import pallas as pl
from jax.experimental.pallas import tpu as pltpu
from jax.sharding import PartitionSpec as P

EPSILON = 1e-05
CHUNKS = 6
ROWS_Y = 2
UP, DOWN, SIDE = 0, 1, 2
MESH = pl.DeviceIdType.MESH


def kernel(
    hid_count, wid_count,
    tok_hbm, gain_hbm, qw_hbm, qs_hbm, kw_hbm, ks_hbm, keys_hbm, vals_hbm, len_ref,
    att_ref, new_ref,
    gat, gain, qw, qs, kw, ks, keys, vals,
    stat_mine, stat_other, stats, normed, acc, acc_rx, kv_acc, kv_rx, kv_new,
    q_tx, q_rx, q_f32, o_f32, att,
    tok_sem, qw_sem, kw_sem, misc_sem,
    send_sem, recv_sem, pair_sem, acc_send, acc_recv, q_send, q_recv, out_sem,
):
    own_rows, half_width = tok_hbm.shape
    full_width = half_width * wid_count
    width = half_width // CHUNKS
    tiles, _, _, req, head_dim = acc.shape
    z_count = hid_count // ROWS_Y
    me = lax.axis_index("hid")
    core = lax.axis_index("wid")
    other = 1 - core
    z = me // ROWS_Y
    y = lax.rem(me, ROWS_Y)
    side = z * ROWS_Y + (1 - y)

    def hid_at(zz, yy):
        return zz * ROWS_Y + yy

    def cols(c):
        return pl.ds(pl.multiple_of(c * width, 128), width)

    def tok_copy(c):
        return pltpu.make_async_copy(tok_hbm.at[:, cols(c)], gat.at[me, c], tok_sem.at[c])

    def kw_copy(c):
        return pltpu.make_async_copy(kw_hbm.at[cols(c)], kw.at[c], kw_sem.at[c])

    def qw_copy(c):
        return pltpu.make_async_copy(qw_hbm.at[cols(c)], qw.at[c], qw_sem.at[c])

    small = [
        pltpu.make_async_copy(gain_hbm, gain, misc_sem.at[0]),
        pltpu.make_async_copy(qs_hbm, qs, misc_sem.at[1]),
        pltpu.make_async_copy(ks_hbm, ks, misc_sem.at[2]),
        pltpu.make_async_copy(keys_hbm, keys, misc_sem.at[3]),
        pltpu.make_async_copy(vals_hbm, vals, misc_sem.at[4]),
    ]
    for c in range(CHUNKS):
        tok_copy(c).start()
    for copy in small[:3]:
        copy.start()

    barrier = pltpu.get_barrier_semaphore()

    @pl.when(z + 1 < z_count)
    def _():
        pl.semaphore_signal(barrier, inc=1, device_id={"hid": hid_at(z + 1, y)}, device_id_type=MESH)

    @pl.when(z > 0)
    def _():
        pl.semaphore_signal(barrier, inc=1, device_id={"hid": hid_at(z - 1, y)}, device_id_type=MESH)

    pl.semaphore_signal(barrier, inc=1, device_id={"hid": side}, device_id_type=MESH)
    pl.semaphore_signal(barrier, inc=1, device_id={"wid": other}, device_id_type=MESH)
    for c in range(CHUNKS):
        kw_copy(c).start()
    for c in range(CHUNKS):
        qw_copy(c).start()
    for copy in small[3:]:
        copy.start()

    def block_at(h, c):
        return stats.at[h] if isinstance(c, int) and c == CHUNKS else gat.at[h, c]

    def send(h, c, link, src=None):
        if link == UP:
            target = hid_at(z + 1, y)
        elif link == DOWN:
            target = hid_at(z - 1, y)
        else:
            target = side
        place = block_at(h, c)
        return pltpu.make_async_remote_copy(
            src_ref=place if src is None else src, dst_ref=place,
            send_sem=send_sem.at[link, h, c], recv_sem=recv_sem.at[h, c],
            device_id={"hid": target}, device_id_type=MESH,
        )

    def arrived(h, c):
        pltpu.make_async_remote_copy(
            src_ref=block_at(h, c), dst_ref=block_at(h, c),
            send_sem=send_sem.at[SIDE, h, c], recv_sem=recv_sem.at[h, c],
            device_id={"hid": side}, device_id_type=MESH,
        ).wait_recv()

    def pair(src, dst, k):
        return pltpu.make_async_remote_copy(
            src_ref=src, dst_ref=dst, send_sem=pair_sem.at[0, k], recv_sem=pair_sem.at[1, k],
            device_id={"wid": other}, device_id_type=MESH,
        )

    def own_sends(c, act):
        src = stats.at[me] if isinstance(c, int) and c == CHUNKS else tok_hbm.at[:, cols(c)]

        @pl.when(z + 1 < z_count)
        def _():
            act(send(me, c, UP, src))

        @pl.when(z > 0)
        def _():
            act(send(me, c, DOWN, src))

        act(send(me, c, SIDE, src))

    start = lambda copy: copy.start()
    ends = (z == 0).astype(jnp.int32) + (z == z_count - 1).astype(jnp.int32)
    pl.semaphore_wait(barrier, 4 - ends)
    own_sends(0, start)
    own_sends(1, start)

    row_sum = jnp.zeros((own_rows, 1), jnp.float32)
    row_squares = jnp.zeros((own_rows, 1), jnp.float32)
    for c in range(CHUNKS):
        tok_copy(c).wait()
        block = gat[me, c].astype(jnp.float32)
        row_sum += jnp.sum(block, axis=1, keepdims=True)
        row_squares += jnp.sum(block * block, axis=1, keepdims=True)
    lane = lax.broadcasted_iota(jnp.int32, (own_rows, 128), 1)
    stat_mine[...] = jnp.where(lane < 64, row_sum, row_squares)

    stat_pair = pair(stat_mine, stat_other, 0)
    stat_pair.start()
    stat_pair.wait()
    both = stat_mine[...] + stat_other[...]
    row_mean = both[:, 0:1] / full_width
    variance = both[:, 64:65] / full_width - row_mean * row_mean
    stats[me] = jnp.where(lane < 64, row_mean, lax.rsqrt(variance + EPSILON))
    own_sends(CHUNKS, start)
    for c in range(2, CHUNKS):
        own_sends(c, start)

    for copy in small[:3]:
        copy.wait()

    def normalised(h, c):
        stat = stats[h]
        block = gat[h, c].astype(jnp.float32)
        return ((block - stat[:, 0:1]) * stat[:, 64:65] * gain[:, cols(c)]).astype(jnp.bfloat16)

    kv_acc[...] = jnp.zeros_like(kv_acc)

    def kv_step(c, carry):
        kw_copy(c).wait()
        part = jnp.dot(normalised(me, c), kw[c], preferred_element_type=jnp.float32)
        kv_acc[...] += part.reshape(kv_acc.shape)
        return carry

    lax.fori_loop(0, CHUNKS, kv_step, 0)
    kv_pair = pair(kv_acc.at[other], kv_rx, 1)
    kv_pair.start()

    acc[...] = jnp.zeros_like(acc)

    def sources_at(k, visit):
        @pl.when(z - k >= 0)
        def _():
            visit(z - k, UP)

        @pl.when(z + k < z_count)
        def _():
            visit(z + k, DOWN)

    def for_sources(visit):
        for k in range(1, z_count):
            sources_at(k, visit)

    def onward(h, c, link, act):
        if link == UP:
            @pl.when(z + 1 < z_count)
            def _():
                act(send(h, c, UP))
        else:
            @pl.when(z > 0)
            def _():
                act(send(h, c, DOWN))

    def relay_at(k, c, act, wait):
        def visit(zz, link):
            h = hid_at(zz, y)
            if wait:
                arrived(h, c)
            onward(h, c, link, act)
            act(send(h, c, SIDE))

        sources_at(k, visit)

    def relay_last_side(c, act, wait):
        if wait:
            arrived(side, c)
        onward(side, c, UP, act)
        onward(side, c, DOWN, act)

    def relay_last_at(k, c, act, wait):
        def visit(zz, link):
            for yy in (y, 1 - y):
                h = hid_at(zz, yy)
                if wait:
                    arrived(h, c)
                onward(h, c, link, act)

        sources_at(k, visit)

    def arrived_side(c):
        arrived(side, c)

        def visit(zz, link):
            arrived(hid_at(zz, 1 - y), c)

        for_sources(visit)

    def normalise_all(c):
        def one(h, carry):
            normed[pl.ds(pl.multiple_of(h * own_rows, own_rows), own_rows), :] = normalised(h, c)
            return carry

        lax.fori_loop(0, hid_count, one, 0)

    def product(c, n):
        columns = pl.ds(pl.multiple_of(n * head_dim, head_dim), head_dim)
        part = jnp.dot(normed[...], qw[c, :, columns], preferred_element_type=jnp.float32)
        return part.reshape(acc.shape[1:])

    def compute(c):
        normalise_all(c)
        qw_copy(c).wait()

        def one(n, carry):
            acc[n] += product(c, n)
            return carry

        lax.fori_loop(0, tiles, one, 0)

    last = CHUNKS - 1
    final = last + z_count - 2
    for step in range(final + 1):
        done = step - (z_count - 1)
        if step == final:
            arrived_side(done)
            compute(done)
        if step < z_count - 1:
            relay_at(step + 1, CHUNKS, start, True)
        for k in range(1, z_count):
            c = step - (k - 1)
            if 0 <= c < last:
                relay_at(k, c, start, True)
            elif c == last:
                relay_last_at(k, c, start, True)
        if step == min(2, last - 1):
            relay_last_side(last, start, True)
        if step == z_count - 2:
            arrived_side(CHUNKS)
        if 0 <= done < last - 1:
            arrived_side(done)
            compute(done)
        if step == z_count - 1:
            kv_pair.wait()
            kv_new[...] = ((kv_acc[core] + kv_rx[...]) * ks[...]).astype(jnp.bfloat16)
            new_out = pltpu.make_async_copy(kv_new, new_ref, out_sem.at[0])
            new_out.start()

    def acc_copy(n):
        return pltpu.make_async_remote_copy(
            src_ref=acc.at[n, :, other], dst_ref=acc_rx.at[n],
            send_sem=acc_send.at[n], recv_sem=acc_recv.at[n],
            device_id={"wid": other}, device_id_type=MESH,
        )

    def q_copy(n, d):
        target = lax.rem(me + d, hid_count)
        return pltpu.make_async_remote_copy(
            src_ref=q_tx.at[n, target], dst_ref=q_rx.at[me * tiles + n],
            send_sem=q_send.at[n, d], recv_sem=q_recv.at[me * tiles + n],
            device_id={"hid": target}, device_id_type=MESH,
        )

    def q_arrived(h, n):
        pltpu.make_async_remote_copy(
            src_ref=q_tx.at[n, h], dst_ref=q_rx.at[h * tiles + n],
            send_sem=q_send.at[n, 0], recv_sem=q_recv.at[h * tiles + n],
            device_id={"hid": side}, device_id_type=MESH,
        ).wait_recv()

    normalise_all(last)
    qw_copy(last).wait()
    for n in range(tiles):
        acc[n] += product(last, n)
        acc_copy(n).start()
    for n in range(tiles):
        acc_copy(n).wait_recv()
        total = acc[n, :, core] + acc_rx[n]
        scale = qs[:, pl.ds(n * head_dim, head_dim)]
        q_tx[n] = (total * scale[None]).astype(jnp.bfloat16)
        for d in range(1, hid_count):
            q_copy(n, d).start()
        q_rx[me * tiles + n] = q_tx[n, me]

    finish = lambda copy: copy.wait_send()

    def drain(c, carry):
        own_sends(c, finish)
        return carry

    lax.fori_loop(0, CHUNKS, drain, 0)
    own_sends(CHUNKS, finish)

    def drain_relay(c, carry):
        for k in range(1, z_count):
            relay_at(k, c, finish, False)
        return carry

    lax.fori_loop(0, last, drain_relay, 0)
    relay_last_side(last, finish, False)
    for k in range(1, z_count):
        relay_at(k, CHUNKS, finish, False)
        relay_last_at(k, last, finish, False)
    for copy in small[3:]:
        copy.wait()

    for n in range(tiles):
        for d in range(1, hid_count):
            q_arrived(lax.rem(me + d, hid_count), n)

    heads = hid_count * tiles
    cache_len = keys.shape[1]
    inv_root = head_dim ** (-0.5)
    q_f32[...] = q_rx[...].astype(jnp.float32)
    position = lax.broadcasted_iota(jnp.int32, (heads, cache_len), 1)
    entries = kv_new[...].astype(jnp.float32)
    for r in range(req):
        query = q_f32[:, r, :]
        score = lax.dot_general(
            query.astype(jnp.bfloat16), keys[r], (((1,), (1,)), ((), ())),
            preferred_element_type=jnp.float32,
        ) * inv_root
        score = jnp.where(position < len_ref[r], score, -jnp.inf)
        own = jnp.sum(query * entries[r : r + 1, :head_dim], axis=1, keepdims=True) * inv_root
        peak = jnp.maximum(jnp.max(score, axis=1, keepdims=True), own)
        weight = jnp.exp(score - peak)
        own_weight = jnp.exp(own - peak)
        denom = jnp.sum(weight, axis=1, keepdims=True) + own_weight
        weight = (weight / denom).astype(jnp.bfloat16)
        own_weight = (own_weight / denom).astype(jnp.bfloat16).astype(jnp.float32)
        mixed = jnp.dot(weight, vals[r], preferred_element_type=jnp.float32)
        o_f32[:, r, :] = mixed + own_weight * entries[r : r + 1, head_dim:]
    for h in range(heads):
        att[:, h * head_dim : (h + 1) * head_dim] = o_f32[h].astype(jnp.bfloat16)
    att_out = pltpu.make_async_copy(att, att_ref, out_sem.at[1])
    att_out.start()
    for n in range(tiles):
        acc_copy(n).wait_send()
        for d in range(1, hid_count):
            q_copy(n, d).wait_send()
    new_out.wait()
    att_out.wait()


def body(
    tokens, norm_gain, query_weight, query_scale, kv_weight, kv_scale,
    keys_cache, values_cache, lengths,
):
    hid_count = lax.axis_size("hid")
    wid_count = lax.axis_size("wid")
    own_rows, half_width = tokens.shape
    local_cols = query_weight.shape[1]
    req, cache_len, head_dim = keys_cache.shape
    tiles = local_cols // head_dim
    heads = hid_count * tiles
    width = half_width // CHUNKS
    kv_cols = kv_weight.shape[1]
    bf16, f32 = jnp.bfloat16, jnp.float32
    dma = pltpu.SemaphoreType.DMA
    vm = pltpu.VMEM
    scratch = [
        vm((hid_count, CHUNKS, own_rows, width), bf16),
        vm((1, half_width), f32),
        vm((CHUNKS, width, local_cols), bf16),
        vm((1, local_cols), f32),
        vm((CHUNKS, width, kv_cols), bf16),
        vm((1, kv_cols), f32),
        vm(keys_cache.shape, bf16),
        vm(values_cache.shape, bf16),
        vm((own_rows, 128), f32),
        vm((own_rows, 128), f32),
        vm((hid_count, own_rows, 128), f32),
        vm((hid_count * own_rows, width), bf16),
        vm((tiles, hid_count, wid_count, req, head_dim), f32),
        vm((tiles, hid_count, req, head_dim), f32),
        vm((wid_count, req, kv_cols), f32),
        vm((req, kv_cols), f32),
        vm((req, kv_cols), bf16),
        vm((tiles, hid_count, req, head_dim), bf16),
        vm((heads, req, head_dim), bf16),
        vm((heads, req, head_dim), f32),
        vm((heads, req, head_dim), f32),
        vm((req, heads * head_dim), bf16),
        dma((CHUNKS,)),
        dma((CHUNKS,)),
        dma((CHUNKS,)),
        dma((5,)),
        dma((3, hid_count, CHUNKS + 1)),
        dma((hid_count, CHUNKS + 1)),
        dma((2, 2)),
        dma((tiles,)),
        dma((tiles,)),
        dma((tiles, hid_count)),
        dma((heads,)),
        dma((2,)),
    ]
    hbm = pl.BlockSpec(memory_space=pl.ANY)
    return pl.pallas_call(
        functools.partial(kernel, hid_count, wid_count),
        out_shape=(
            jax.ShapeDtypeStruct((req, heads * head_dim), bf16),
            jax.ShapeDtypeStruct((req, kv_cols), bf16),
        ),
        in_specs=[hbm] * 8 + [pl.BlockSpec(memory_space=pltpu.SMEM)],
        out_specs=(hbm, hbm),
        scratch_shapes=scratch,
        compiler_params=pltpu.CompilerParams(
            collective_id=0, has_side_effects=True, vmem_limit_bytes=60 * 1024 * 1024
        ),
    )(
        tokens, norm_gain.reshape(1, -1), query_weight, query_scale.reshape(1, -1),
        kv_weight, kv_scale.reshape(1, -1), keys_cache, values_cache, lengths,
    )


def solution(mesh):
    placed = (
        P(("groups", "hid"), "wid"),
        P("wid"),
        P("wid", "hid"),
        P("hid"),
        P("wid", None),
        P(),
        P(("groups", "hid", "wid"), None, None),
        P(("groups", "hid", "wid"), None, None),
        P(("groups", "hid", "wid")),
    )
    return jax.shard_map(
        body,
        mesh=mesh,
        in_specs=placed,
        out_specs=(P(("groups", "hid", "wid"), None), P(("groups", "hid", "wid"), None)),
        check_vma=False,
    )
```

```python
import functools

import jax
import jax.numpy as jnp
from jax import lax
from jax.experimental import pallas as pl
from jax.experimental.pallas import tpu as pltpu
from jax.sharding import PartitionSpec as P

EPSILON = 1e-05
CHUNKS = 4
ROWS_Y = 2
UP, DOWN, SIDE = 0, 1, 2
MESH = pl.DeviceIdType.MESH


def kernel(
    hid_count, wid_count,
    tok_hbm, gain_hbm, qw_hbm, qs_hbm, kw_hbm, ks_hbm, keys_hbm, vals_hbm, len_ref,
    att_ref, new_ref,
    gat, gain, qw, qs, kw, ks, keys, vals,
    stat_mine, stat_other, stats, normed, acc, acc_rx, kv_acc, kv_rx, kv_new,
    q_tx, q_rx, q_f32, o_f32, att,
    tok_sem, qw_sem, kw_sem, misc_sem,
    send_sem, recv_sem, pair_sem, acc_send, acc_recv, q_send, q_recv, out_sem,
):
    own_rows, half_width = tok_hbm.shape
    full_width = half_width * wid_count
    width = half_width // CHUNKS
    tiles, _, _, req, head_dim = acc.shape
    z_count = hid_count // ROWS_Y
    me = lax.axis_index("hid")
    core = lax.axis_index("wid")
    other = 1 - core
    z = me // ROWS_Y
    y = lax.rem(me, ROWS_Y)
    side = z * ROWS_Y + (1 - y)

    def hid_at(zz, yy):
        return zz * ROWS_Y + yy

    def cols(c):
        return pl.ds(pl.multiple_of(c * width, 128), width)

    def tok_copy(c):
        return pltpu.make_async_copy(tok_hbm.at[:, cols(c)], gat.at[me, c], tok_sem.at[c])

    def kw_copy(c):
        return pltpu.make_async_copy(kw_hbm.at[cols(c)], kw.at[c], kw_sem.at[c])

    def qw_copy(c):
        return pltpu.make_async_copy(qw_hbm.at[cols(c)], qw.at[c], qw_sem.at[c])

    small = [
        pltpu.make_async_copy(gain_hbm, gain, misc_sem.at[0]),
        pltpu.make_async_copy(qs_hbm, qs, misc_sem.at[1]),
        pltpu.make_async_copy(ks_hbm, ks, misc_sem.at[2]),
        pltpu.make_async_copy(keys_hbm, keys, misc_sem.at[3]),
        pltpu.make_async_copy(vals_hbm, vals, misc_sem.at[4]),
    ]
    for c in range(CHUNKS):
        tok_copy(c).start()
    for copy in small[:3]:
        copy.start()

    barrier = pltpu.get_barrier_semaphore()

    @pl.when(z + 1 < z_count)
    def _():
        pl.semaphore_signal(barrier, inc=1, device_id={"hid": hid_at(z + 1, y)}, device_id_type=MESH)

    @pl.when(z > 0)
    def _():
        pl.semaphore_signal(barrier, inc=1, device_id={"hid": hid_at(z - 1, y)}, device_id_type=MESH)

    pl.semaphore_signal(barrier, inc=1, device_id={"hid": side}, device_id_type=MESH)
    pl.semaphore_signal(barrier, inc=1, device_id={"wid": other}, device_id_type=MESH)
    for c in range(CHUNKS):
        kw_copy(c).start()
    for c in range(CHUNKS):
        qw_copy(c).start()
    for copy in small[3:]:
        copy.start()

    def block_at(h, c):
        return stats.at[h] if isinstance(c, int) and c == CHUNKS else gat.at[h, c]

    def send(h, c, link, src=None):
        if link == UP:
            target = hid_at(z + 1, y)
        elif link == DOWN:
            target = hid_at(z - 1, y)
        else:
            target = side
        place = block_at(h, c)
        return pltpu.make_async_remote_copy(
            src_ref=place if src is None else src, dst_ref=place,
            send_sem=send_sem.at[link, h, c], recv_sem=recv_sem.at[h, c],
            device_id={"hid": target}, device_id_type=MESH,
        )

    def arrived(h, c):
        pltpu.make_async_remote_copy(
            src_ref=block_at(h, c), dst_ref=block_at(h, c),
            send_sem=send_sem.at[SIDE, h, c], recv_sem=recv_sem.at[h, c],
            device_id={"hid": side}, device_id_type=MESH,
        ).wait_recv()

    def pair(src, dst, k):
        return pltpu.make_async_remote_copy(
            src_ref=src, dst_ref=dst, send_sem=pair_sem.at[0, k], recv_sem=pair_sem.at[1, k],
            device_id={"wid": other}, device_id_type=MESH,
        )

    def own_sends(c, act):
        src = stats.at[me] if isinstance(c, int) and c == CHUNKS else tok_hbm.at[:, cols(c)]

        @pl.when(z + 1 < z_count)
        def _():
            act(send(me, c, UP, src))

        @pl.when(z > 0)
        def _():
            act(send(me, c, DOWN, src))

        act(send(me, c, SIDE, src))

    start = lambda copy: copy.start()
    ends = (z == 0).astype(jnp.int32) + (z == z_count - 1).astype(jnp.int32)
    pl.semaphore_wait(barrier, 4 - ends)
    for c in range(CHUNKS):
        own_sends(c, start)

    row_sum = jnp.zeros((own_rows, 1), jnp.float32)
    row_squares = jnp.zeros((own_rows, 1), jnp.float32)
    for c in range(CHUNKS):
        tok_copy(c).wait()
        block = gat[me, c].astype(jnp.float32)
        row_sum += jnp.sum(block, axis=1, keepdims=True)
        row_squares += jnp.sum(block * block, axis=1, keepdims=True)
    lane = lax.broadcasted_iota(jnp.int32, (own_rows, 128), 1)
    stat_mine[...] = jnp.where(lane < 64, row_sum, row_squares)

    stat_pair = pair(stat_mine, stat_other, 0)
    stat_pair.start()
    stat_pair.wait()
    both = stat_mine[...] + stat_other[...]
    row_mean = both[:, 0:1] / full_width
    variance = both[:, 64:65] / full_width - row_mean * row_mean
    stats[me] = jnp.where(lane < 64, row_mean, lax.rsqrt(variance + EPSILON))
    own_sends(CHUNKS, start)

    for copy in small[:3]:
        copy.wait()

    def normalised(h, c):
        stat = stats[h]
        block = gat[h, c].astype(jnp.float32)
        return ((block - stat[:, 0:1]) * stat[:, 64:65] * gain[:, cols(c)]).astype(jnp.bfloat16)

    kv_acc[...] = jnp.zeros_like(kv_acc)

    def kv_step(c, carry):
        kw_copy(c).wait()
        part = jnp.dot(normalised(me, c), kw[c], preferred_element_type=jnp.float32)
        kv_acc[...] += part.reshape(kv_acc.shape)
        return carry

    kv_pair = pair(kv_acc.at[other], kv_rx, 1)
    acc[...] = jnp.zeros_like(acc)

    def sources_at(k, visit):
        @pl.when(z - k >= 0)
        def _():
            visit(z - k, UP)

        @pl.when(z + k < z_count)
        def _():
            visit(z + k, DOWN)

    def for_sources(visit):
        for k in range(1, z_count):
            sources_at(k, visit)

    def onward(h, c, link, act):
        if link == UP:
            @pl.when(z + 1 < z_count)
            def _():
                act(send(h, c, UP))
        else:
            @pl.when(z > 0)
            def _():
                act(send(h, c, DOWN))

    def relay_at(k, c, act, wait):
        def visit(zz, link):
            h = hid_at(zz, y)
            if wait:
                arrived(h, c)
            onward(h, c, link, act)
            act(send(h, c, SIDE))

        sources_at(k, visit)

    def relay_last_side(c, act, wait):
        if wait:
            arrived(side, c)
        onward(side, c, UP, act)
        onward(side, c, DOWN, act)

    def relay_last_at(k, c, act, wait):
        def visit(zz, link):
            for yy in (y, 1 - y):
                h = hid_at(zz, yy)
                if wait:
                    arrived(h, c)
                onward(h, c, link, act)

        sources_at(k, visit)

    def arrived_side(c):
        arrived(side, c)

        def visit(zz, link):
            arrived(hid_at(zz, 1 - y), c)

        for_sources(visit)

    def normalise_all(c):
        def one(h, carry):
            normed[pl.ds(pl.multiple_of(h * own_rows, own_rows), own_rows), :] = normalised(h, c)
            return carry

        lax.fori_loop(0, hid_count, one, 0)

    def product(c, n):
        columns = pl.ds(pl.multiple_of(n * head_dim, head_dim), head_dim)
        part = jnp.dot(normed[...], qw[c, :, columns], preferred_element_type=jnp.float32)
        return part.reshape(acc.shape[1:])

    def compute(c):
        normalise_all(c)
        qw_copy(c).wait()

        def one(n, carry):
            acc[n] += product(c, n)
            return carry

        lax.fori_loop(0, tiles, one, 0)

    last = CHUNKS - 1
    final = last + z_count - 2
    for step in range(final + 1):
        done = step - (z_count - 1)
        if step == final:
            arrived_side(done)
            compute(done)
        for k in range(1, z_count):
            c = step - (k - 1)
            if 0 <= c < last:
                relay_at(k, c, start, True)
            elif c == last:
                relay_last_at(k, c, start, True)
        if step == min(2, last - 1):
            relay_last_side(last, start, True)
        if step < CHUNKS // 2:
            lax.fori_loop(2 * step, 2 * step + 2, kv_step, 0)
        if step == CHUNKS // 2 - 1:
            kv_pair.start()
        if 1 <= step < z_count:
            relay_at(step, CHUNKS, start, True)
        if step == z_count - 1:
            arrived_side(CHUNKS)
        if 0 <= done < last - 1:
            arrived_side(done)
            compute(done)
        if step == max(z_count - 1, CHUNKS // 2):
            kv_pair.wait()
            kv_new[...] = ((kv_acc[core] + kv_rx[...]) * ks[...]).astype(jnp.bfloat16)
            new_out = pltpu.make_async_copy(kv_new, new_ref, out_sem.at[0])
            new_out.start()

    def acc_copy(n):
        return pltpu.make_async_remote_copy(
            src_ref=acc.at[n, :, other], dst_ref=acc_rx.at[n],
            send_sem=acc_send.at[n], recv_sem=acc_recv.at[n],
            device_id={"wid": other}, device_id_type=MESH,
        )

    def q_copy(n, d):
        target = lax.rem(me + d, hid_count)
        return pltpu.make_async_remote_copy(
            src_ref=q_tx.at[n, target], dst_ref=q_rx.at[me * tiles + n],
            send_sem=q_send.at[n, d], recv_sem=q_recv.at[me * tiles + n],
            device_id={"hid": target}, device_id_type=MESH,
        )

    def q_arrived(h, n):
        pltpu.make_async_remote_copy(
            src_ref=q_tx.at[n, h], dst_ref=q_rx.at[h * tiles + n],
            send_sem=q_send.at[n, 0], recv_sem=q_recv.at[h * tiles + n],
            device_id={"hid": side}, device_id_type=MESH,
        ).wait_recv()

    normalise_all(last)
    qw_copy(last).wait()
    for n in range(tiles):
        acc[n] += product(last, n)
        acc_copy(n).start()
    for n in range(tiles):
        acc_copy(n).wait_recv()
        total = acc[n, :, core] + acc_rx[n]
        scale = qs[:, pl.ds(n * head_dim, head_dim)]
        q_tx[n] = (total * scale[None]).astype(jnp.bfloat16)
        for d in range(1, hid_count):
            q_copy(n, d).start()
        q_rx[me * tiles + n] = q_tx[n, me]

    finish = lambda copy: copy.wait_send()

    def drain(c, carry):
        own_sends(c, finish)
        return carry

    lax.fori_loop(0, CHUNKS, drain, 0)
    own_sends(CHUNKS, finish)

    def drain_relay(c, carry):
        for k in range(1, z_count):
            relay_at(k, c, finish, False)
        return carry

    lax.fori_loop(0, last, drain_relay, 0)
    relay_last_side(last, finish, False)
    for k in range(1, z_count):
        relay_at(k, CHUNKS, finish, False)
        relay_last_at(k, last, finish, False)
    for copy in small[3:]:
        copy.wait()

    for n in range(tiles):
        for d in range(1, hid_count):
            q_arrived(lax.rem(me + d, hid_count), n)

    heads = hid_count * tiles
    cache_len = keys.shape[1]
    inv_root = head_dim ** (-0.5)
    q_f32[...] = q_rx[...].astype(jnp.float32)
    position = lax.broadcasted_iota(jnp.int32, (heads, cache_len), 1)
    entries = kv_new[...].astype(jnp.float32)
    for r in range(req):
        query = q_f32[:, r, :]
        score = lax.dot_general(
            query.astype(jnp.bfloat16), keys[r], (((1,), (1,)), ((), ())),
            preferred_element_type=jnp.float32,
        ) * inv_root
        score = jnp.where(position < len_ref[r], score, -jnp.inf)
        own = jnp.sum(query * entries[r : r + 1, :head_dim], axis=1, keepdims=True) * inv_root
        peak = jnp.maximum(jnp.max(score, axis=1, keepdims=True), own)
        weight = jnp.exp(score - peak)
        own_weight = jnp.exp(own - peak)
        denom = jnp.sum(weight, axis=1, keepdims=True) + own_weight
        weight = (weight / denom).astype(jnp.bfloat16)
        own_weight = (own_weight / denom).astype(jnp.bfloat16).astype(jnp.float32)
        mixed = jnp.dot(weight, vals[r], preferred_element_type=jnp.float32)
        o_f32[:, r, :] = mixed + own_weight * entries[r : r + 1, head_dim:]
    for h in range(heads):
        att[:, h * head_dim : (h + 1) * head_dim] = o_f32[h].astype(jnp.bfloat16)
    att_out = pltpu.make_async_copy(att, att_ref, out_sem.at[1])
    att_out.start()
    for n in range(tiles):
        acc_copy(n).wait_send()
        for d in range(1, hid_count):
            q_copy(n, d).wait_send()
    new_out.wait()
    att_out.wait()


def hand_on(att_ref, new_ref, att_out, new_out):
    att_out[...] = att_ref[...]
    new_out[...] = new_ref[...]


def body(
    tokens, norm_gain, query_weight, query_scale, kv_weight, kv_scale,
    keys_cache, values_cache, lengths,
):
    hid_count = lax.axis_size("hid")
    wid_count = lax.axis_size("wid")
    own_rows, half_width = tokens.shape
    local_cols = query_weight.shape[1]
    req, cache_len, head_dim = keys_cache.shape
    tiles = local_cols // head_dim
    heads = hid_count * tiles
    width = half_width // CHUNKS
    kv_cols = kv_weight.shape[1]
    bf16, f32 = jnp.bfloat16, jnp.float32
    dma = pltpu.SemaphoreType.DMA
    vm = pltpu.VMEM
    scratch = [
        vm((hid_count, CHUNKS, own_rows, width), bf16),
        vm((1, half_width), f32),
        vm((CHUNKS, width, local_cols), bf16),
        vm((1, local_cols), f32),
        vm((CHUNKS, width, kv_cols), bf16),
        vm((1, kv_cols), f32),
        vm(keys_cache.shape, bf16),
        vm(values_cache.shape, bf16),
        vm((own_rows, 128), f32),
        vm((own_rows, 128), f32),
        vm((hid_count, own_rows, 128), f32),
        vm((hid_count * own_rows, width), bf16),
        vm((tiles, hid_count, wid_count, req, head_dim), f32),
        vm((tiles, hid_count, req, head_dim), f32),
        vm((wid_count, req, kv_cols), f32),
        vm((req, kv_cols), f32),
        vm((req, kv_cols), bf16),
        vm((tiles, hid_count, req, head_dim), bf16),
        vm((heads, req, head_dim), bf16),
        vm((heads, req, head_dim), f32),
        vm((heads, req, head_dim), f32),
        vm((req, heads * head_dim), bf16),
        dma((CHUNKS,)),
        dma((CHUNKS,)),
        dma((CHUNKS,)),
        dma((5,)),
        dma((3, hid_count, CHUNKS + 1)),
        dma((hid_count, CHUNKS + 1)),
        dma((2, 2)),
        dma((tiles,)),
        dma((tiles,)),
        dma((tiles, hid_count)),
        dma((heads,)),
        dma((2,)),
    ]
    hbm = pl.BlockSpec(memory_space=pl.ANY)
    attended, new_entries = pl.pallas_call(
        functools.partial(kernel, hid_count, wid_count),
        out_shape=(
            jax.ShapeDtypeStruct((req, heads * head_dim), bf16),
            jax.ShapeDtypeStruct((req, kv_cols), bf16),
        ),
        in_specs=[hbm] * 8 + [pl.BlockSpec(memory_space=pltpu.SMEM)],
        out_specs=(hbm, hbm),
        scratch_shapes=scratch,
        compiler_params=pltpu.CompilerParams(
            collective_id=0, has_side_effects=True, vmem_limit_bytes=60 * 1024 * 1024
        ),
    )(
        tokens, norm_gain.reshape(1, -1), query_weight, query_scale.reshape(1, -1),
        kv_weight, kv_scale.reshape(1, -1), keys_cache, values_cache, lengths,
    )
    whole = pl.BlockSpec(memory_space=pltpu.VMEM)
    return pl.pallas_call(
        hand_on,
        out_shape=(
            jax.ShapeDtypeStruct(attended.shape, bf16),
            jax.ShapeDtypeStruct(new_entries.shape, bf16),
        ),
        in_specs=[whole, whole],
        out_specs=(whole, whole),
    )(attended, new_entries)


def solution(mesh):
    placed = (
        P(("groups", "hid"), "wid"),
        P("wid"),
        P("wid", "hid"),
        P("hid"),
        P("wid", None),
        P(),
        P(("groups", "hid", "wid"), None, None),
        P(("groups", "hid", "wid"), None, None),
        P(("groups", "hid", "wid")),
    )
    return jax.shard_map(
        body,
        mesh=mesh,
        in_specs=placed,
        out_specs=(P(("groups", "hid", "wid"), None), P(("groups", "hid", "wid"), None)),
        check_vma=False,
    )
```
